32 devices in a mesh: case: 2 (over y), panel: 4 (over z), slab: 2 (over x), obs: 2 (over core).
Axes of the slice: x: 2, y: 2, z: 4, core: 2. Of those that a mesh axis runs over, the one named last changes fastest.
Arguments:
- loading: bfloat16 [65536, 512], P(('case', 'panel'), 'slab'), parts along dimension 0, may hold values from -6 to 6
- green: bfloat16 [128, 32768], P(('case', 'obs'), 'panel'), parts along dimension 0, may hold values from -0.03125 to 0.03125
- delays: int32 [128, 2048], P(('case', 'obs'), 'panel'), parts along dimension 0, may hold values from 0 to 120
- offsets: int32 [128, 2048], P(('case', 'obs'), 'panel'), parts along dimension 0, may hold values from 0 to 7
- live_groups: int32 [8], P('case'), parts along dimension 0, may hold values from 1 to 4, as said below
Outputs:
- signal: float32 [128, 512], P(('case', 'obs'), 'slab'), parts along dimension 0
The draws below stay inside these ranges and needn't reach their ends.
There are 2 independent parts, one for each index of `case`. The reference program is written for one: setup_inputs(seed, part) draws one part's arguments, and reference() takes and returns one part's arrays. A program takes and returns all parts, laid end to end along the dimension named above; each array names one. Nothing has to cross between parts.
Inputs may be any that keep to these rules, and one draw needn't show every extreme that they name: `live_groups`: in every draw some sector has all 4 groups live while the sector 4/2 positions away has one.
All inputs are finite; a program needn't handle non-finite values.
Results may differ from the reference program's by a relative error of at most 0.0034.
Values may be sent and summed in bfloat16 or wider, within the bound.
A program may use at most 64 MiB of HBM per device.

```python
import jax
import jax.numpy as jnp
from jax import lax

OBS = 64
BP = 16
GB = 128
GROUPS = 4
LAGS = 128
SECTORS = 4
PANELS = 32768
BLOCKS = 2048
TSAMP = 512


def draw_live_groups(key, part):
    first_key, second_key, third_key = jax.random.split(jax.random.fold_in(key, 17), 3)
    heavy = jax.random.randint(first_key, (SECTORS,), 0, 3) == 0
    extra = jax.random.randint(second_key, (SECTORS,), 2, GROUPS + 1)
    counts = jnp.where(heavy, extra, 1).astype(jnp.int32)
    picked = jax.random.randint(third_key, (), 0, SECTORS)
    counts = counts.at[picked].set(GROUPS)
    partner = jnp.bitwise_xor(picked, SECTORS // 2)
    counts = counts.at[partner].set(1)
    return counts.astype(jnp.int32)


def touch_ends(entries, stream_key, least, high):
    longest = entries.shape.index(max(entries.shape))
    spots = []
    for shift in (0, 1):
        where = [jax.random.randint(jax.random.fold_in(stream_key, axis), (), 0, length) for axis, length in enumerate(entries.shape)]
        where[longest] = (where[longest] + shift) % entries.shape[longest]
        spots.append(tuple(where))
    return entries.at[spots[0]].set(least).at[spots[1]].set(high)


def level_of(stream_key, shape, shards, smallest, largest):
    factor_of, own = 1.0, jax.random.fold_in(stream_key, 6)
    for axis_at, blocks in shards:
        steps = jnp.exp(jax.random.uniform(jax.random.fold_in(own, axis_at), (blocks,), jnp.float32, smallest / len(shards), largest / len(shards)))
        factor_of = factor_of * jnp.repeat(steps, shape[axis_at] // blocks).reshape([-1 if axis == axis_at else 1 for axis in range(len(shape))])
    return factor_of


def normal_values(key, shape, spread, reach, pieces=(), kind=jnp.bfloat16):
    level = level_of(key, shape, pieces, -0.22, 0.18) if pieces else 1.0
    values = jax.random.normal(key, shape, jnp.float32) * spread * level
    return jnp.minimum(jnp.maximum(values, -reach), reach).astype(kind)


def setup_inputs(seed: int = 0, part: int = 0) -> dict:
    arg_keys = jax.random.split(jax.random.key(seed), 6)
    own_keys = jax.random.split(jax.random.fold_in(arg_keys[5], part), 6)
    loading = normal_values(own_keys[0], (PANELS, TSAMP), 1.0, 6.0, ((0, 4), (1, 2)))
    green = normal_values(own_keys[1], (OBS, PANELS), PANELS ** -0.5, 0.03125, ((0, 2), (1, 4)))
    delays = touch_ends(jax.random.randint(own_keys[2], (OBS, BLOCKS), 0, LAGS - 7), jax.random.fold_in(own_keys[2], 1), 0, (LAGS - 7) - 1).astype(jnp.int32)
    offsets = touch_ends(jax.random.randint(own_keys[3], (OBS, BLOCKS), 0, 8), jax.random.fold_in(own_keys[3], 1), 0, 7).astype(jnp.int32)
    live_groups = draw_live_groups(jax.random.fold_in(jax.random.fold_in(arg_keys[5], part), 71), part)
    return dict(loading=loading, green=green, delays=delays, offsets=offsets, live_groups=live_groups)


def lagrange_weights(offset_part):
    position = 3.0 + offset_part.astype(jnp.float32) / 8.0
    weights = []
    for tap in range(8):
        factor = jnp.ones_like(position)
        for other in range(8):
            if other != tap:
                factor = factor * (position - other) / (tap - other)
        weights.append(factor)
    return weights


def build_table(delay_part, offset_part, lag_count):
    lag_index = jnp.arange(lag_count, dtype=jnp.int32)[None, :, None]
    relative = lag_index - delay_part.astype(jnp.int32)[:, None, :]
    weights = lagrange_weights(offset_part)
    table_sum = jnp.zeros(relative.shape, jnp.float32)
    for tap in range(8):
        table_sum = table_sum + jnp.where(relative == tap, weights[tap][:, None, :], 0.0)
    return table_sum.astype(jnp.bfloat16)


def reference(loading, green, delays, offsets, live_groups):
    samples = loading.shape[1]
    group_count = SECTORS * GROUPS
    grouped_load = loading.reshape(group_count, GB, BP, samples)
    grouped_green = jnp.moveaxis(green.reshape(OBS, group_count, GB, BP), 1, 0)
    grouped_delay = jnp.moveaxis(delays.reshape(OBS, group_count, GB), 1, 0)
    grouped_offset = jnp.moveaxis(offsets.reshape(OBS, group_count, GB), 1, 0)
    fft_length = samples + LAGS

    def compute(group_index):
        block_signal = jnp.einsum("obp,bpt->bot", grouped_green[group_index].astype(jnp.float32),
                                  grouped_load[group_index].astype(jnp.float32)).astype(jnp.bfloat16)
        block_signal = lax.optimization_barrier(block_signal).astype(jnp.float32)
        lag_table = build_table(grouped_delay[group_index], grouped_offset[group_index], LAGS)
        lag_table = lax.optimization_barrier(lag_table).astype(jnp.float32)
        signal_spectrum = jnp.fft.rfft(block_signal, fft_length, axis=2)
        table_spectrum = jnp.fft.rfft(jnp.transpose(lag_table, (2, 0, 1)), fft_length, axis=2)
        combined = jnp.sum(signal_spectrum * table_spectrum, axis=0)
        return jnp.fft.irfft(combined, fft_length, axis=1)[:, :samples].astype(jnp.float32)

    def skipped(group_index):
        return jnp.zeros((OBS, samples), jnp.float32)

    def step_group(carried, group_index):
        sector = group_index // GROUPS
        is_live = live_groups[sector] > group_index % GROUPS
        return carried + lax.cond(is_live, compute, skipped, group_index), None

    start_sum = jnp.zeros((OBS, samples), jnp.float32)
    signal, unused = lax.scan(step_group, start_sum, jnp.arange(group_count, dtype=jnp.int32))
    return signal
```

```python
import functools
import math

import jax
import jax.numpy as jnp
from jax import lax
from jax.experimental import pallas as pl
from jax.experimental.pallas import tpu as pltpu
from jax.sharding import PartitionSpec as P

BP = 16
GB = 128
LAGS = 128
TAPS = 8
STEPS = 8
KT = 256
LANES = 128
ROWS = 8
SHARES = (4, 28)
BEFORE = 8
MESH = pl.DeviceIdType.MESH


def kernel(panels, slabs, live_hbm, load_hbm, green_hbm, delay_hbm, offset_hbm, out_ref,
           live_ref, load_ref, green_ref, delay_ref, offset_ref, table_ref, block_ref, wide_ref, part_ref,
           main_out, tail_out, main_in, tail_in, load_sem, green_sem, small_sem, main_send, main_recv, tail_send, tail_recv):
    panel = lax.axis_index("panel")
    slab = lax.axis_index("slab")
    n_panels, samples = load_hbm.shape
    observers = green_hbm.shape[0]
    blocks = delay_hbm.shape[1]
    chunks = observers // ROWS
    tiles = n_panels // KT
    wide = samples // LANES
    across = blocks // LANES
    edges = [tiles * sum(SHARES[:c]) // sum(SHARES) for c in range(len(SHARES) + 1)]
    has_next = slab < slabs - 1
    has_prev = slab > 0

    smalls = [pltpu.make_async_copy(src, dst, small_sem.at[i]) for i, (src, dst) in enumerate(
        ((delay_hbm, delay_ref), (offset_hbm, offset_ref), (live_hbm, live_ref)))]
    for copy in smalls:
        copy.start()
    greens, loads = [], []
    for c in range(len(SHARES)):
        rows = pl.ds(edges[c] * KT, (edges[c + 1] - edges[c]) * KT)
        greens.append(pltpu.make_async_copy(green_hbm.at[:, rows], green_ref.at[:, rows], green_sem.at[c]))
        greens[-1].start()
        loads.append(pltpu.make_async_copy(load_hbm.at[rows, :], load_ref.at[rows, :], load_sem.at[c]))
        loads[-1].start()

    barrier = pltpu.get_barrier_semaphore()
    for d in range(1, panels):
        pl.semaphore_signal(barrier, inc=1, device_id={"panel": lax.rem(panel + d, panels)}, device_id_type=MESH)

    @pl.when(has_next)
    def _():
        for d in range(panels):
            pl.semaphore_signal(barrier, inc=1, device_id={
                "panel": lax.rem(panel + d, panels), "slab": slab + 1}, device_id_type=MESH)

    @pl.when(has_prev)
    def _():
        for d in range(panels):
            pl.semaphore_signal(barrier, inc=1, device_id={
                "panel": lax.rem(panel + d, panels), "slab": slab - 1}, device_id_type=MESH)

    lane = lax.broadcasted_iota(jnp.int32, (ROWS, LANES), 1)
    row8 = lax.broadcasted_iota(jnp.int32, (ROWS, LANES), 0)
    lane16 = lax.broadcasted_iota(jnp.int32, (BP, LANES), 1)
    row16 = lax.broadcasted_iota(jnp.int32, (BP, LANES), 0)
    diagonal = jnp.where(lane16 // BP == row16 % ROWS, 1.0, 0.0).astype(jnp.bfloat16)
    empty = jnp.zeros((BP, LANES), jnp.bfloat16)

    position = 3.0 + (lane // TAPS).astype(jnp.float32) * 0.125
    tap_of = lane % TAPS
    choice = jnp.ones((ROWS, LANES), jnp.float32)
    below = jnp.ones((ROWS, LANES), jnp.float32)
    for m in range(TAPS):
        here = tap_of == m
        choice = choice * jnp.where(here, 1.0, position - float(m))
        below = below * jnp.where(here, 1.0, (tap_of - m).astype(jnp.float32))
    choice = choice / below

    for copy in smalls:
        copy.wait()
    live = live_ref[panel]
    group_of = lax.broadcasted_iota(jnp.int32, (observers, blocks), 1) // GB
    delay_ref[...] = jnp.where(group_of < live, delay_ref[...], 4 * LAGS)
    offset_ref[...] = offset_ref[...] * TAPS

    def table_step(o):
        for a in range(across):
            lanes = slice(a * LANES, (a + 1) * LANES)
            delay = jnp.broadcast_to(delay_ref[o:o + 1, lanes], (ROWS, LANES))
            step = jnp.broadcast_to(offset_ref[o:o + 1, lanes], (ROWS, LANES))
            which = step + ((row8 - delay) & (ROWS - 1))
            stencil = jnp.take_along_axis(choice, which, axis=1, mode="promise_in_bounds")
            place = ((delay + (ROWS - 1) - row8) >> 3).astype(jnp.float32)
            place = jnp.concatenate([place, place - 1.0], axis=0).astype(jnp.bfloat16)
            stencil = jnp.concatenate([stencil, stencil], axis=0).astype(jnp.bfloat16)
            for q in range(LAGS // BP):
                table_ref[o, q * BP:(q + 1) * BP, lanes] = jnp.where(
                    place == jnp.bfloat16(2 * q), stencil, jnp.bfloat16(0))

    def widen_step(tile):
        columns = slice(tile * KT, (tile + 1) * KT)
        wide_ref[:, columns] = green_ref[:, columns].astype(jnp.float32)

    def spread_step(first, last, tile):
        pieces = []
        for o in range(first, last, 2):
            for h in range(KT // LANES):
                lanes = slice(tile * KT + h * LANES, tile * KT + (h + 1) * LANES)
                pair = jnp.concatenate([
                    jnp.broadcast_to(wide_ref[i:i + 1, lanes], (ROWS, LANES)) for i in (o, o + 1)], axis=0)
                pair = pair.astype(jnp.bfloat16) * diagonal
                pieces.append(jnp.concatenate([pair if i == h else empty for i in range(KT // LANES)], axis=1))
        product = jnp.dot(jnp.concatenate(pieces, axis=0), load_ref[tile * KT:(tile + 1) * KT, :],
                          preferred_element_type=jnp.float32)
        for o in range(first, last, 2):
            for i in range(2):
                start = (o - first) * BP + i * ROWS
                rows = jnp.concatenate([product[start + h * BP:start + h * BP + ROWS] for h in range(KT // LANES)], axis=0)
                block_ref[o + i, tile * BP:(tile + 1) * BP, :] = rows.astype(jnp.bfloat16)

    def lag_step(o):
        return jnp.dot(table_ref[o], block_ref[o], preferred_element_type=jnp.float32)

    def shift(parts, amount):
        keep = lane >= amount
        rolled = [None if part is None else pltpu.roll(part, amount, 1) for part in parts]
        moved = [jnp.where(keep, rolled[0], 0.0)]
        for j in range(1, len(parts)):
            moved.append(jnp.where(keep, 0.0 if rolled[j] is None else rolled[j], rolled[j - 1]))
        return moved

    def add(left, right):
        return [l if r is None else l + r for l, r in zip(left, right)]

    def fold(lagged):
        total = [lagged[:ROWS, j * LANES:(j + 1) * LANES] for j in range(wide)] + [None]
        for h in range(1, LAGS // ROWS):
            parts = [lagged[h * ROWS:(h + 1) * ROWS, j * LANES:(j + 1) * LANES] for j in range(wide)] + [None]
            total = add(shift(parts, h * ROWS), total)
        return total

    def merge(left, right, bit):
        clear = (row8 & bit) == 0
        stay, move = [], []
        for a, b in zip(left, right):
            stay.append(jnp.where(clear, a, pltpu.roll(b, bit, 0)))
            move.append(jnp.where(clear, pltpu.roll(a, ROWS - bit, 0), b))
        return add(shift(move, bit), stay)

    def gather(folded):
        bit = ROWS // 2
        while len(folded) > 1:
            half = len(folded) // 2
            folded = [merge(folded[i], folded[i + half], bit) for i in range(half)]
            bit //= 2
        return folded[0]

    def main_copy(c, d):
        return pltpu.make_async_remote_copy(
            src_ref=main_out.at[c],
            dst_ref=main_in.at[c, d - 1],
            send_sem=main_send.at[c, d - 1], recv_sem=main_recv.at[c, d - 1],
            device_id={"panel": lax.rem(panel + d, panels)}, device_id_type=MESH)

    def tail_copy(c, d):
        return pltpu.make_async_remote_copy(
            src_ref=tail_out.at[c],
            dst_ref=tail_in.at[c, d],
            send_sem=tail_send.at[c, d], recv_sem=tail_recv.at[c, d],
            device_id={"panel": lax.rem(panel + d, panels), "slab": slab + 1}, device_id_type=MESH)

    def keep(c, gathered):
        for j in range(wide):
            lanes = slice(j * LANES, (j + 1) * LANES)
            part_ref[c * ROWS:(c + 1) * ROWS, lanes] = gathered[j]
            main_out[c, :, lanes] = gathered[j].astype(jnp.bfloat16)
        tail_out[c] = gathered[wide].astype(jnp.bfloat16)

    def send(c):
        @pl.when(has_next)
        def _():
            for d in range(panels):
                tail_copy(c, d).start()

        for d in range(1, panels):
            main_copy(c, d).start()

    cut = observers - ROWS
    built = BEFORE
    for o in range(BEFORE):
        table_step(o)
    for c in range(len(SHARES)):
        greens[c].wait()
        loads[c].wait()
        for tile in range(edges[c], edges[c + 1]):
            widen_step(tile)
            spread_step(0, cut, tile)
            due = BEFORE + (observers - BEFORE) * (tile + 1) // tiles
            for o in range(built, due):
                table_step(o)
            built = due

    folded = []
    done = 0
    for tile in range(tiles):
        spread_step(cut, observers, tile)
        due = cut * (tile + 1) // tiles
        for o in range(done, due):
            folded.append(fold(lag_step(o)))
            if len(folded) == ROWS:
                keep(o // ROWS, gather(folded))
                folded = []
        done = due
    pl.semaphore_wait(barrier, panels - 1 + panels * (has_next.astype(jnp.int32) + has_prev.astype(jnp.int32)))
    for c in range(cut // ROWS):
        send(c)

    keep(chunks - 1, gather([fold(lag_step(o)) for o in range(cut, observers)]))
    send(chunks - 1)

    for c in range(chunks):
        rows = slice(c * ROWS, (c + 1) * ROWS)
        total = part_ref[rows, :]
        for d in range(1, panels):
            main_copy(c, d).wait_recv()
            total = total + main_in[c, d - 1].astype(jnp.float32)
        out_ref[rows, :] = total

        @pl.when(has_prev)
        def _():
            late = None
            for d in range(panels):
                tail_copy(c, d).wait_recv()
                term = tail_in[c, d].astype(jnp.float32)
                late = term if late is None else late + term
            out_ref[rows, :LAGS] += late

    for c in range(chunks):
        for d in range(1, panels):
            main_copy(c, d).wait_send()

        @pl.when(has_next)
        def _():
            for d in range(panels):
                tail_copy(c, d).wait_send()


def shards(panels, slabs, loading, green, delays, offsets, live_groups):
    n_panels, samples = loading.shape
    observers = green.shape[0]
    blocks = delays.shape[1]
    chunks = observers // ROWS
    peers = max(panels - 1, 1)
    anywhere = pl.BlockSpec(memory_space=pltpu.HBM)
    return pl.pallas_call(
        functools.partial(kernel, panels, slabs),
        out_shape=jax.ShapeDtypeStruct((observers, samples), jnp.float32),
        in_specs=[anywhere] * 5,
        out_specs=pl.BlockSpec(memory_space=pltpu.VMEM),
        scratch_shapes=[
            pltpu.SMEM((panels,), jnp.int32),
            pltpu.VMEM((n_panels, samples), jnp.bfloat16),
            pltpu.VMEM((observers, n_panels), jnp.bfloat16),
            pltpu.VMEM((observers, blocks), jnp.int32),
            pltpu.VMEM((observers, blocks), jnp.int32),
            pltpu.VMEM((observers, LAGS, blocks), jnp.bfloat16),
            pltpu.VMEM((observers, blocks, samples), jnp.bfloat16),
            pltpu.VMEM((observers, n_panels), jnp.float32),
            pltpu.VMEM((observers, samples), jnp.float32),
            pltpu.VMEM((chunks, ROWS, samples), jnp.bfloat16),
            pltpu.VMEM((chunks, ROWS, LAGS), jnp.bfloat16),
            pltpu.VMEM((chunks, peers, ROWS, samples), jnp.bfloat16),
            pltpu.VMEM((chunks, panels, ROWS, LAGS), jnp.bfloat16),
            pltpu.SemaphoreType.DMA((len(SHARES),)),
            pltpu.SemaphoreType.DMA((len(SHARES),)),
            pltpu.SemaphoreType.DMA((3,)),
            pltpu.SemaphoreType.DMA((chunks, peers)),
            pltpu.SemaphoreType.DMA((chunks, peers)),
            pltpu.SemaphoreType.DMA((chunks, panels)),
            pltpu.SemaphoreType.DMA((chunks, panels)),
        ],
        compiler_params=pltpu.CompilerParams(
            collective_id=0, has_side_effects=True, vmem_limit_bytes=40 * 2 ** 20),
        name="far_field",
    )(*(pltpu.with_memory_space_constraint(x, pltpu.HBM) for x in (live_groups, loading, green, delays, offsets)))


def solution(mesh):
    placed = (
        P(("case", "panel"), "slab"),
        P(("case", "obs"), "panel"),
        P(("case", "obs"), "panel"),
        P(("case", "obs"), "panel"),
        P("case"),
    )
    return jax.shard_map(
        functools.partial(shards, mesh.shape["panel"], mesh.shape["slab"]),
        mesh=mesh, in_specs=placed, out_specs=P(("case", "obs"), "slab"), check_vma=False,
    )
```

```python
import functools
import math

import jax
import jax.numpy as jnp
from jax import lax
from jax.experimental import pallas as pl
from jax.experimental.pallas import tpu as pltpu
from jax.sharding import PartitionSpec as P

BP = 16
GB = 128
LAGS = 128
TAPS = 8
STEPS = 8
KT = 256
LANES = 128
ROWS = 8
SHARES = (4, 12, 16)
TABLES = (8, 8, 8)
LATE = 8
MESH = pl.DeviceIdType.MESH


def kernel(panels, slabs, live_hbm, load_hbm, green_hbm, delay_hbm, offset_hbm, out_ref,
           live_ref, load_ref, green_ref, delay_ref, offset_ref, table_ref, block_ref, wide_ref, part_ref,
           main_out, tail_out, main_in, tail_in, load_sem, green_sem, small_sem, main_send, main_recv, tail_send, tail_recv):
    panel = lax.axis_index("panel")
    slab = lax.axis_index("slab")
    n_panels, samples = load_hbm.shape
    observers = green_hbm.shape[0]
    blocks = delay_hbm.shape[1]
    tiles = n_panels // KT
    wide = samples // LANES
    across = blocks // LANES
    edges = [tiles * sum(SHARES[:c]) // sum(SHARES) for c in range(len(SHARES) + 1)]
    has_next = slab < slabs - 1
    has_prev = slab > 0

    smalls = [pltpu.make_async_copy(src, dst, small_sem.at[i]) for i, (src, dst) in enumerate(
        ((delay_hbm, delay_ref), (offset_hbm, offset_ref), (live_hbm, live_ref)))]
    for copy in smalls:
        copy.start()
    greens, loads = [], []
    for c in range(len(SHARES)):
        rows = pl.ds(edges[c] * KT, (edges[c + 1] - edges[c]) * KT)
        greens.append(pltpu.make_async_copy(green_hbm.at[:, rows], green_ref.at[:, rows], green_sem.at[c]))
        greens[-1].start()
        loads.append(pltpu.make_async_copy(load_hbm.at[rows, :], load_ref.at[rows, :], load_sem.at[c]))
        loads[-1].start()

    barrier = pltpu.get_barrier_semaphore()
    for d in range(1, panels):
        pl.semaphore_signal(barrier, inc=1, device_id={"panel": lax.rem(panel + d, panels)}, device_id_type=MESH)

    @pl.when(has_next)
    def _():
        for d in range(panels):
            pl.semaphore_signal(barrier, inc=1, device_id={
                "panel": lax.rem(panel + d, panels), "slab": slab + 1}, device_id_type=MESH)

    @pl.when(has_prev)
    def _():
        for d in range(panels):
            pl.semaphore_signal(barrier, inc=1, device_id={
                "panel": lax.rem(panel + d, panels), "slab": slab - 1}, device_id_type=MESH)

    lane = lax.broadcasted_iota(jnp.int32, (ROWS, LANES), 1)
    row8 = lax.broadcasted_iota(jnp.int32, (ROWS, LANES), 0)
    lane16 = lax.broadcasted_iota(jnp.int32, (BP, LANES), 1)
    row16 = lax.broadcasted_iota(jnp.int32, (BP, LANES), 0)
    diagonal = jnp.where(lane16 // BP == row16 % ROWS, 1.0, 0.0).astype(jnp.bfloat16)
    empty = jnp.zeros((BP, LANES), jnp.bfloat16)

    position = 3.0 + (lane // TAPS).astype(jnp.float32) * 0.125
    tap_of = lane % TAPS
    choice = jnp.ones((ROWS, LANES), jnp.float32)
    below = jnp.ones((ROWS, LANES), jnp.float32)
    for m in range(TAPS):
        here = tap_of == m
        choice = choice * jnp.where(here, 1.0, position - float(m))
        below = below * jnp.where(here, 1.0, (tap_of - m).astype(jnp.float32))
    choice = choice / below

    for copy in smalls:
        copy.wait()
    live = live_ref[panel]
    group_of = lax.broadcasted_iota(jnp.int32, (observers, blocks), 1) // GB
    delay_ref[...] = jnp.where(group_of < live, delay_ref[...], 4 * LAGS)
    offset_ref[...] = offset_ref[...] * TAPS

    def table_step(o):
        stencils, places = [], []
        for a in range(across):
            lanes = slice(a * LANES, (a + 1) * LANES)
            delay = jnp.broadcast_to(delay_ref[o:o + 1, lanes], (ROWS, LANES))
            step = jnp.broadcast_to(offset_ref[o:o + 1, lanes], (ROWS, LANES))
            which = step + ((row8 - delay) & (ROWS - 1))
            stencils.append(jnp.take_along_axis(choice, which, axis=1, mode="promise_in_bounds"))
            places.append(((delay + (ROWS - 1) - row8) >> 3).astype(jnp.float32))
        stencil = jnp.concatenate(stencils, axis=1).astype(jnp.bfloat16)
        place = jnp.concatenate(places, axis=1).astype(jnp.bfloat16)
        for q in range(LAGS // ROWS):
            table_ref[o, q * ROWS:(q + 1) * ROWS, :] = jnp.where(place == jnp.bfloat16(q), stencil, jnp.bfloat16(0))

    def widen_step(tile):
        columns = slice(tile * KT, (tile + 1) * KT)
        wide_ref[:, columns] = green_ref[:, columns].astype(jnp.float32)

    def spread_step(first, last, tile):
        pieces = []
        for o in range(first, last, 2):
            for h in range(KT // LANES):
                lanes = slice(tile * KT + h * LANES, tile * KT + (h + 1) * LANES)
                pair = jnp.concatenate([
                    jnp.broadcast_to(wide_ref[i:i + 1, lanes], (ROWS, LANES)) for i in (o, o + 1)], axis=0)
                pair = pair.astype(jnp.bfloat16) * diagonal
                pieces.append(jnp.concatenate([pair if i == h else empty for i in range(KT // LANES)], axis=1))
        product = jnp.dot(jnp.concatenate(pieces, axis=0), load_ref[tile * KT:(tile + 1) * KT, :],
                          preferred_element_type=jnp.float32)
        for o in range(first, last, 2):
            for i in range(2):
                start = (o - first) * BP + i * ROWS
                rows = jnp.concatenate([product[start + h * BP:start + h * BP + ROWS] for h in range(KT // LANES)], axis=0)
                block_ref[o + i, tile * BP:(tile + 1) * BP, :] = rows.astype(jnp.bfloat16)

    def lag_step(o):
        return jnp.dot(table_ref[o], block_ref[o], preferred_element_type=jnp.float32)

    def shift(parts, amount):
        keep = lane >= amount
        rolled = [None if part is None else pltpu.roll(part, amount, 1) for part in parts]
        moved = [jnp.where(keep, rolled[0], 0.0)]
        for j in range(1, len(parts)):
            moved.append(jnp.where(keep, 0.0 if rolled[j] is None else rolled[j], rolled[j - 1]))
        return moved

    def add(left, right):
        return [l if r is None else l + r for l, r in zip(left, right)]

    def fold(lagged):
        total = [lagged[:ROWS, j * LANES:(j + 1) * LANES] for j in range(wide)] + [None]
        for h in range(1, LAGS // ROWS):
            parts = [lagged[h * ROWS:(h + 1) * ROWS, j * LANES:(j + 1) * LANES] for j in range(wide)] + [None]
            total = add(shift(parts, h * ROWS), total)
        return total

    def merge(left, right, bit):
        clear = (row8 & bit) == 0
        stay, move = [], []
        for a, b in zip(left, right):
            stay.append(jnp.where(clear, a, pltpu.roll(b, bit, 0)))
            move.append(jnp.where(clear, pltpu.roll(a, ROWS - bit, 0), b))
        return add(shift(move, bit), stay)

    def gather(folded):
        bit = ROWS // 2
        while len(folded) > 1:
            half = len(folded) // 2
            folded = [merge(folded[i], folded[i + half], bit) for i in range(half)]
            bit //= 2
        return folded[0]

    spans = ((0, observers - LATE), (observers - LATE, observers))

    def main_copy(c, d):
        rows = slice(*spans[c])
        return pltpu.make_async_remote_copy(
            src_ref=main_out.at[rows],
            dst_ref=main_in.at[d - 1, rows],
            send_sem=main_send.at[c, d - 1], recv_sem=main_recv.at[c, d - 1],
            device_id={"panel": lax.rem(panel + d, panels)}, device_id_type=MESH)

    def tail_copy(c, d):
        rows = slice(*spans[c])
        return pltpu.make_async_remote_copy(
            src_ref=tail_out.at[rows],
            dst_ref=tail_in.at[d, rows],
            send_sem=tail_send.at[c, d], recv_sem=tail_recv.at[c, d],
            device_id={"panel": lax.rem(panel + d, panels), "slab": slab + 1}, device_id_type=MESH)

    def sum_rows(first):
        gathered = gather([fold(lag_step(o)) for o in range(first, first + ROWS)])
        rows = slice(first, first + ROWS)
        for j in range(wide):
            lanes = slice(j * LANES, (j + 1) * LANES)
            part_ref[rows, lanes] = gathered[j]
            main_out[rows, lanes] = gathered[j].astype(jnp.bfloat16)
        tail_out[rows, :] = gathered[wide].astype(jnp.bfloat16)

    def send(c):
        for d in range(1, panels):
            main_copy(c, d).start()

        @pl.when(has_next)
        def _():
            for d in range(panels):
                tail_copy(c, d).start()

    built = 0

    def tables_step(count):
        nonlocal built
        for o in range(built, min(built + count, observers)):
            table_step(o)
        built = min(built + count, observers)

    tables_step(TABLES[0])
    for c in range(len(SHARES)):
        greens[c].wait()
        loads[c].wait()
        for tile in range(edges[c], edges[c + 1]):
            widen_step(tile)
            spread_step(0, observers, tile)
        tables_step(TABLES[c + 1] if c + 1 < len(SHARES) else observers)

    for c in range(len(spans)):
        for first in range(spans[c][0], spans[c][1], ROWS):
            sum_rows(first)
        if c == 0:
            pl.semaphore_wait(barrier, panels - 1 + panels * (has_next.astype(jnp.int32) + has_prev.astype(jnp.int32)))
        send(c)

    for c in range(len(spans)):
        rows = slice(*spans[c])
        total = part_ref[rows, :]
        for d in range(1, panels):
            main_copy(c, d).wait_recv()
            total = total + main_in[d - 1, rows, :].astype(jnp.float32)
        out_ref[rows, :] = total

        @pl.when(has_prev)
        def _():
            late = None
            for d in range(panels):
                tail_copy(c, d).wait_recv()
                term = tail_in[d, rows, :].astype(jnp.float32)
                late = term if late is None else late + term
            out_ref[rows, :LAGS] += late

    for c in range(len(spans)):
        for d in range(1, panels):
            main_copy(c, d).wait_send()

        @pl.when(has_next)
        def _():
            for d in range(panels):
                tail_copy(c, d).wait_send()


def shards(panels, slabs, loading, green, delays, offsets, live_groups):
    n_panels, samples = loading.shape
    observers = green.shape[0]
    blocks = delays.shape[1]
    peers = max(panels - 1, 1)
    anywhere = pl.BlockSpec(memory_space=pltpu.HBM)
    return pl.pallas_call(
        functools.partial(kernel, panels, slabs),
        out_shape=jax.ShapeDtypeStruct((observers, samples), jnp.float32),
        in_specs=[anywhere] * 5,
        out_specs=pl.BlockSpec(memory_space=pltpu.VMEM),
        scratch_shapes=[
            pltpu.SMEM((panels,), jnp.int32),
            pltpu.VMEM((n_panels, samples), jnp.bfloat16),
            pltpu.VMEM((observers, n_panels), jnp.bfloat16),
            pltpu.VMEM((observers, blocks), jnp.int32),
            pltpu.VMEM((observers, blocks), jnp.int32),
            pltpu.VMEM((observers, LAGS, blocks), jnp.bfloat16),
            pltpu.VMEM((observers, blocks, samples), jnp.bfloat16),
            pltpu.VMEM((observers, n_panels), jnp.float32),
            pltpu.VMEM((observers, samples), jnp.float32),
            pltpu.VMEM((observers, samples), jnp.bfloat16),
            pltpu.VMEM((observers, LAGS), jnp.bfloat16),
            pltpu.VMEM((peers, observers, samples), jnp.bfloat16),
            pltpu.VMEM((panels, observers, LAGS), jnp.bfloat16),
            pltpu.SemaphoreType.DMA((len(SHARES),)),
            pltpu.SemaphoreType.DMA((len(SHARES),)),
            pltpu.SemaphoreType.DMA((3,)),
            pltpu.SemaphoreType.DMA((2, peers)),
            pltpu.SemaphoreType.DMA((2, peers)),
            pltpu.SemaphoreType.DMA((2, panels)),
            pltpu.SemaphoreType.DMA((2, panels)),
        ],
        compiler_params=pltpu.CompilerParams(
            collective_id=0, has_side_effects=True, vmem_limit_bytes=40 * 2 ** 20),
        name="far_field",
    )(*(pltpu.with_memory_space_constraint(x, pltpu.HBM) for x in (live_groups, loading, green, delays, offsets)))


def solution(mesh):
    placed = (
        P(("case", "panel"), "slab"),
        P(("case", "obs"), "panel"),
        P(("case", "obs"), "panel"),
        P(("case", "obs"), "panel"),
        P("case"),
    )
    return jax.shard_map(
        functools.partial(shards, mesh.shape["panel"], mesh.shape["slab"]),
        mesh=mesh, in_specs=placed, out_specs=P(("case", "obs"), "slab"), check_vma=False,
    )
```

```python
import functools
import math

import jax
import jax.numpy as jnp
from jax import lax
from jax.experimental import pallas as pl
from jax.experimental.pallas import tpu as pltpu
from jax.sharding import PartitionSpec as P

BP = 16
GB = 128
LAGS = 128
TAPS = 8
STEPS = 8
KT = 256
LANES = 128
ROWS = 8
SHARES = (4, 12, 16)
TABLES = (1, 1, 1, 1)
EVERY = 99
LATE = 8
MESH = pl.DeviceIdType.MESH


def kernel(panels, slabs, live_hbm, load_hbm, green_hbm, delay_hbm, offset_hbm, out_ref,
           live_ref, load_ref, green_ref, delay_ref, offset_ref, table_ref, block_ref, wide_ref, part_ref,
           main_out, tail_out, main_in, tail_in, load_sem, green_sem, small_sem, main_send, main_recv, tail_send, tail_recv):
    panel = lax.axis_index("panel")
    slab = lax.axis_index("slab")
    n_panels, samples = load_hbm.shape
    observers = green_hbm.shape[0]
    blocks = delay_hbm.shape[1]
    tiles = n_panels // KT
    wide = samples // LANES
    across = blocks // LANES
    edges = [tiles * sum(SHARES[:c]) // sum(SHARES) for c in range(len(SHARES) + 1)]
    has_next = slab < slabs - 1
    has_prev = slab > 0

    smalls = [pltpu.make_async_copy(src, dst, small_sem.at[i]) for i, (src, dst) in enumerate(
        ((delay_hbm, delay_ref), (offset_hbm, offset_ref), (live_hbm, live_ref)))]
    for copy in smalls:
        copy.start()
    greens, loads = [], []
    for c in range(len(SHARES)):
        rows = pl.ds(edges[c] * KT, (edges[c + 1] - edges[c]) * KT)
        greens.append(pltpu.make_async_copy(green_hbm.at[:, rows], green_ref.at[:, rows], green_sem.at[c]))
        greens[-1].start()
        loads.append(pltpu.make_async_copy(load_hbm.at[rows, :], load_ref.at[rows, :], load_sem.at[c]))
        loads[-1].start()

    barrier = pltpu.get_barrier_semaphore()
    for d in range(1, panels):
        pl.semaphore_signal(barrier, inc=1, device_id={"panel": lax.rem(panel + d, panels)}, device_id_type=MESH)

    @pl.when(has_next)
    def _():
        for d in range(panels):
            pl.semaphore_signal(barrier, inc=1, device_id={
                "panel": lax.rem(panel + d, panels), "slab": slab + 1}, device_id_type=MESH)

    @pl.when(has_prev)
    def _():
        for d in range(panels):
            pl.semaphore_signal(barrier, inc=1, device_id={
                "panel": lax.rem(panel + d, panels), "slab": slab - 1}, device_id_type=MESH)

    lane = lax.broadcasted_iota(jnp.int32, (ROWS, LANES), 1)
    row8 = lax.broadcasted_iota(jnp.int32, (ROWS, LANES), 0)
    lane16 = lax.broadcasted_iota(jnp.int32, (BP, LANES), 1)
    row16 = lax.broadcasted_iota(jnp.int32, (BP, LANES), 0)
    diagonal = jnp.where(lane16 // BP == row16 % ROWS, 1.0, 0.0).astype(jnp.bfloat16)
    empty = jnp.zeros((BP, LANES), jnp.bfloat16)

    position = 3.0 + (lane // TAPS).astype(jnp.float32) * 0.125
    tap_of = lane % TAPS
    choice = jnp.ones((ROWS, LANES), jnp.float32)
    below = jnp.ones((ROWS, LANES), jnp.float32)
    for m in range(TAPS):
        here = tap_of == m
        choice = choice * jnp.where(here, 1.0, position - float(m))
        below = below * jnp.where(here, 1.0, (tap_of - m).astype(jnp.float32))
    choice = choice / below

    for copy in smalls:
        copy.wait()
    live = live_ref[panel]
    group_of = lax.broadcasted_iota(jnp.int32, (observers, blocks), 1) // GB
    delay_ref[...] = jnp.where(group_of < live, delay_ref[...], 4 * LAGS)
    offset_ref[...] = offset_ref[...] * TAPS

    stored = [o for o in range(observers) if o >= observers - LATE or o % EVERY == 0]

    def entries(o, a):
        lanes = slice(a * LANES, (a + 1) * LANES)
        delay = jnp.broadcast_to(delay_ref[o:o + 1, lanes], (ROWS, LANES))
        step = jnp.broadcast_to(offset_ref[o:o + 1, lanes], (ROWS, LANES))
        which = step + ((row8 - delay) & (ROWS - 1))
        stencil = jnp.take_along_axis(choice, which, axis=1, mode="promise_in_bounds")
        return stencil, ((delay + (ROWS - 1) - row8) >> 3).astype(jnp.float32)

    def table_step(o):
        parts = [entries(o, a) for a in range(across)]
        stencil = jnp.concatenate([part[0] for part in parts], axis=1).astype(jnp.bfloat16)
        place = jnp.concatenate([part[1] for part in parts], axis=1).astype(jnp.bfloat16)
        for q in range(LAGS // ROWS):
            table_ref[o, q * ROWS:(q + 1) * ROWS, :] = jnp.where(place == jnp.bfloat16(q), stencil, jnp.bfloat16(0))

    def table_of(o):
        if o in stored:
            return table_ref[o]
        columns = []
        for a in range(across):
            stencil, place = entries(o, a)
            place = jnp.concatenate([place, place - 1.0], axis=0).astype(jnp.bfloat16)
            stencil = jnp.concatenate([stencil, stencil], axis=0).astype(jnp.bfloat16)
            columns.append(jnp.concatenate([
                jnp.where(place == jnp.bfloat16(2 * q), stencil, jnp.bfloat16(0)) for q in range(LAGS // BP)], axis=0))
        return jnp.concatenate(columns, axis=1)

    def widen_step(tile):
        columns = slice(tile * KT, (tile + 1) * KT)
        wide_ref[:, columns] = green_ref[:, columns].astype(jnp.float32)

    def spread_step(first, last, tile):
        pieces = []
        for o in range(first, last, 2):
            for h in range(KT // LANES):
                lanes = slice(tile * KT + h * LANES, tile * KT + (h + 1) * LANES)
                pair = jnp.concatenate([
                    jnp.broadcast_to(wide_ref[i:i + 1, lanes], (ROWS, LANES)) for i in (o, o + 1)], axis=0)
                pair = pair.astype(jnp.bfloat16) * diagonal
                pieces.append(jnp.concatenate([pair if i == h else empty for i in range(KT // LANES)], axis=1))
        product = jnp.dot(jnp.concatenate(pieces, axis=0), load_ref[tile * KT:(tile + 1) * KT, :],
                          preferred_element_type=jnp.float32)
        for o in range(first, last, 2):
            for i in range(2):
                start = (o - first) * BP + i * ROWS
                rows = jnp.concatenate([product[start + h * BP:start + h * BP + ROWS] for h in range(KT // LANES)], axis=0)
                block_ref[o + i, tile * BP:(tile + 1) * BP, :] = rows.astype(jnp.bfloat16)

    def lag_step(o):
        return jnp.dot(table_of(o), block_ref[o], preferred_element_type=jnp.float32)

    def shift(parts, amount):
        keep = lane >= amount
        rolled = [None if part is None else pltpu.roll(part, amount, 1) for part in parts]
        moved = [jnp.where(keep, rolled[0], 0.0)]
        for j in range(1, len(parts)):
            moved.append(jnp.where(keep, 0.0 if rolled[j] is None else rolled[j], rolled[j - 1]))
        return moved

    def add(left, right):
        return [l if r is None else l + r for l, r in zip(left, right)]

    def fold(left, right):
        totals = [[lagged[:ROWS, j * LANES:(j + 1) * LANES] for j in range(wide)] + [None] for lagged in (left, right)]
        for h in range(1, LAGS // ROWS):
            rows = slice(h * ROWS, (h + 1) * ROWS)
            keep = lane16 >= h * ROWS
            rolled = []
            for j in range(wide):
                lanes = slice(j * LANES, (j + 1) * LANES)
                both = jnp.concatenate([left[rows, lanes], right[rows, lanes]], axis=0).astype(jnp.bfloat16)
                rolled.append(pltpu.roll(both, h * ROWS, 1))
            none = jnp.zeros_like(rolled[0])
            moved = [jnp.where(keep, a, b) for a, b in zip(rolled + [none], [none] + rolled)]
            moved = [part.astype(jnp.float32) for part in moved]
            totals = [add([part[i * ROWS:(i + 1) * ROWS] for part in moved], totals[i]) for i in range(2)]
        return totals

    def merge(left, right, bit):
        clear = (row8 & bit) == 0
        stay, move = [], []
        for a, b in zip(left, right):
            stay.append(jnp.where(clear, a, pltpu.roll(b, bit, 0)))
            move.append(jnp.where(clear, pltpu.roll(a, ROWS - bit, 0), b))
        return add(shift(move, bit), stay)

    def gather(folded):
        bit = ROWS // 2
        while len(folded) > 1:
            half = len(folded) // 2
            folded = [merge(folded[i], folded[i + half], bit) for i in range(half)]
            bit //= 2
        return folded[0]

    spans = ((0, observers - LATE), (observers - LATE, observers))

    def main_copy(c, d):
        rows = slice(*spans[c])
        return pltpu.make_async_remote_copy(
            src_ref=main_out.at[rows],
            dst_ref=main_in.at[d - 1, rows],
            send_sem=main_send.at[c, d - 1], recv_sem=main_recv.at[c, d - 1],
            device_id={"panel": lax.rem(panel + d, panels)}, device_id_type=MESH)

    def tail_copy(c, d):
        rows = slice(*spans[c])
        return pltpu.make_async_remote_copy(
            src_ref=tail_out.at[rows],
            dst_ref=tail_in.at[d, rows],
            send_sem=tail_send.at[c, d], recv_sem=tail_recv.at[c, d],
            device_id={"panel": lax.rem(panel + d, panels), "slab": slab + 1}, device_id_type=MESH)

    def sum_rows(first):
        folded = []
        for o in range(first, first + ROWS, 2):
            folded += fold(lag_step(o), lag_step(o + 1))
        gathered = gather(folded)
        rows = slice(first, first + ROWS)
        for j in range(wide):
            lanes = slice(j * LANES, (j + 1) * LANES)
            part_ref[rows, lanes] = gathered[j]
            main_out[rows, lanes] = gathered[j].astype(jnp.bfloat16)
        tail_out[rows, :] = gathered[wide].astype(jnp.bfloat16)

    def send(c):
        for d in range(1, panels):
            main_copy(c, d).start()

        @pl.when(has_next)
        def _():
            for d in range(panels):
                tail_copy(c, d).start()

    waiting = list(stored)
    for c in range(len(SHARES)):
        for o in waiting[:len(stored) * TABLES[c] // sum(TABLES)]:
            table_step(o)
            waiting.remove(o)
        greens[c].wait()
        loads[c].wait()
        for tile in range(edges[c], edges[c + 1]):
            widen_step(tile)
            spread_step(0, observers, tile)
    for o in waiting:
        table_step(o)

    for c in range(len(spans)):
        for first in range(spans[c][0], spans[c][1], ROWS):
            sum_rows(first)
        if c == 0:
            pl.semaphore_wait(barrier, panels - 1 + panels * (has_next.astype(jnp.int32) + has_prev.astype(jnp.int32)))
        send(c)

    for c in range(len(spans)):
        rows = slice(*spans[c])
        total = part_ref[rows, :]
        for d in range(1, panels):
            main_copy(c, d).wait_recv()
            total = total + main_in[d - 1, rows, :].astype(jnp.float32)
        out_ref[rows, :] = total

        @pl.when(has_prev)
        def _():
            late = None
            for d in range(panels):
                tail_copy(c, d).wait_recv()
                term = tail_in[d, rows, :].astype(jnp.float32)
                late = term if late is None else late + term
            out_ref[rows, :LAGS] += late

    for c in range(len(spans)):
        for d in range(1, panels):
            main_copy(c, d).wait_send()

        @pl.when(has_next)
        def _():
            for d in range(panels):
                tail_copy(c, d).wait_send()


def shards(panels, slabs, loading, green, delays, offsets, live_groups):
    n_panels, samples = loading.shape
    observers = green.shape[0]
    blocks = delays.shape[1]
    peers = max(panels - 1, 1)
    anywhere = pl.BlockSpec(memory_space=pltpu.HBM)
    return pl.pallas_call(
        functools.partial(kernel, panels, slabs),
        out_shape=jax.ShapeDtypeStruct((observers, samples), jnp.float32),
        in_specs=[anywhere] * 5,
        out_specs=pl.BlockSpec(memory_space=pltpu.VMEM),
        scratch_shapes=[
            pltpu.SMEM((panels,), jnp.int32),
            pltpu.VMEM((n_panels, samples), jnp.bfloat16),
            pltpu.VMEM((observers, n_panels), jnp.bfloat16),
            pltpu.VMEM((observers, blocks), jnp.int32),
            pltpu.VMEM((observers, blocks), jnp.int32),
            pltpu.VMEM((observers, LAGS, blocks), jnp.bfloat16),
            pltpu.VMEM((observers, blocks, samples), jnp.bfloat16),
            pltpu.VMEM((observers, n_panels), jnp.float32),
            pltpu.VMEM((observers, samples), jnp.float32),
            pltpu.VMEM((observers, samples), jnp.bfloat16),
            pltpu.VMEM((observers, LAGS), jnp.bfloat16),
            pltpu.VMEM((peers, observers, samples), jnp.bfloat16),
            pltpu.VMEM((panels, observers, LAGS), jnp.bfloat16),
            pltpu.SemaphoreType.DMA((len(SHARES),)),
            pltpu.SemaphoreType.DMA((len(SHARES),)),
            pltpu.SemaphoreType.DMA((3,)),
            pltpu.SemaphoreType.DMA((2, peers)),
            pltpu.SemaphoreType.DMA((2, peers)),
            pltpu.SemaphoreType.DMA((2, panels)),
            pltpu.SemaphoreType.DMA((2, panels)),
        ],
        compiler_params=pltpu.CompilerParams(
            collective_id=0, has_side_effects=True, vmem_limit_bytes=40 * 2 ** 20),
        name="far_field",
    )(*(pltpu.with_memory_space_constraint(x, pltpu.HBM) for x in (live_groups, loading, green, delays, offsets)))


def solution(mesh):
    placed = (
        P(("case", "panel"), "slab"),
        P(("case", "obs"), "panel"),
        P(("case", "obs"), "panel"),
        P(("case", "obs"), "panel"),
        P("case"),
    )
    return jax.shard_map(
        functools.partial(shards, mesh.shape["panel"], mesh.shape["slab"]),
        mesh=mesh, in_specs=placed, out_specs=P(("case", "obs"), "slab"), check_vma=False,
    )
```

```python
import functools
import math

import jax
import jax.numpy as jnp
from jax import lax
from jax.experimental import pallas as pl
from jax.experimental.pallas import tpu as pltpu
from jax.sharding import PartitionSpec as P

BP = 16
GB = 128
LAGS = 128
TAPS = 8
STEPS = 8
KT = 256
LANES = 128
ROWS = 8
SHARES = (4, 12, 16)
TABLES = (1, 1, 1, 1)
LATE = 8
MESH = pl.DeviceIdType.MESH


def kernel(panels, slabs, live_hbm, load_hbm, green_hbm, delay_hbm, offset_hbm, out_ref,
           live_ref, load_ref, green_ref, delay_ref, offset_ref, table_ref, block_ref, wide_ref, part_ref,
           main_out, tail_out, main_in, tail_in, load_sem, green_sem, small_sem, main_send, main_recv, tail_send, tail_recv):
    panel = lax.axis_index("panel")
    slab = lax.axis_index("slab")
    n_panels, samples = load_hbm.shape
    observers = green_hbm.shape[0]
    blocks = delay_hbm.shape[1]
    tiles = n_panels // KT
    wide = samples // LANES
    across = blocks // LANES
    edges = [tiles * sum(SHARES[:c]) // sum(SHARES) for c in range(len(SHARES) + 1)]
    has_next = slab < slabs - 1
    has_prev = slab > 0

    smalls = [pltpu.make_async_copy(src, dst, small_sem.at[i]) for i, (src, dst) in enumerate(
        ((delay_hbm, delay_ref), (offset_hbm, offset_ref), (live_hbm, live_ref)))]
    for copy in smalls:
        copy.start()
    greens, loads = [], []
    for c in range(len(SHARES)):
        rows = pl.ds(edges[c] * KT, (edges[c + 1] - edges[c]) * KT)
        greens.append(pltpu.make_async_copy(green_hbm.at[:, rows], green_ref.at[:, rows], green_sem.at[c]))
        greens[-1].start()
        loads.append(pltpu.make_async_copy(load_hbm.at[rows, :], load_ref.at[rows, :], load_sem.at[c]))
        loads[-1].start()

    barrier = pltpu.get_barrier_semaphore()
    for d in range(1, panels):
        pl.semaphore_signal(barrier, inc=1, device_id={"panel": lax.rem(panel + d, panels)}, device_id_type=MESH)

    @pl.when(has_next)
    def _():
        for d in range(panels):
            pl.semaphore_signal(barrier, inc=1, device_id={
                "panel": lax.rem(panel + d, panels), "slab": slab + 1}, device_id_type=MESH)

    @pl.when(has_prev)
    def _():
        for d in range(panels):
            pl.semaphore_signal(barrier, inc=1, device_id={
                "panel": lax.rem(panel + d, panels), "slab": slab - 1}, device_id_type=MESH)

    lane = lax.broadcasted_iota(jnp.int32, (ROWS, LANES), 1)
    row8 = lax.broadcasted_iota(jnp.int32, (ROWS, LANES), 0)
    lane16 = lax.broadcasted_iota(jnp.int32, (BP, LANES), 1)
    row16 = lax.broadcasted_iota(jnp.int32, (BP, LANES), 0)
    diagonal = jnp.where(lane16 // BP == row16 % ROWS, 1.0, 0.0).astype(jnp.bfloat16)
    empty = jnp.zeros((BP, LANES), jnp.bfloat16)

    position = 3.0 + (lane // TAPS).astype(jnp.float32) * 0.125
    tap_of = lane % TAPS
    choice = jnp.ones((ROWS, LANES), jnp.float32)
    below = jnp.ones((ROWS, LANES), jnp.float32)
    for m in range(TAPS):
        here = tap_of == m
        choice = choice * jnp.where(here, 1.0, position - float(m))
        below = below * jnp.where(here, 1.0, (tap_of - m).astype(jnp.float32))
    choice = choice / below

    for copy in smalls:
        copy.wait()
    live = live_ref[panel]
    group_of = lax.broadcasted_iota(jnp.int32, (observers, blocks), 1) // GB
    delay_ref[...] = jnp.where(group_of < live, delay_ref[...], 4 * LAGS)
    offset_ref[...] = offset_ref[...] * TAPS

    stored = [o for o in range(observers) if o == 0 or o >= observers - LATE]

    def entries(o, a):
        lanes = slice(a * LANES, (a + 1) * LANES)
        delay = jnp.broadcast_to(delay_ref[o:o + 1, lanes], (ROWS, LANES))
        step = jnp.broadcast_to(offset_ref[o:o + 1, lanes], (ROWS, LANES))
        which = step + ((row8 - delay) & (ROWS - 1))
        stencil = jnp.take_along_axis(choice, which, axis=1, mode="promise_in_bounds")
        return stencil, ((delay + (ROWS - 1) - row8) >> 3).astype(jnp.float32)

    def table_step(o):
        parts = [entries(o, a) for a in range(across)]
        stencil = jnp.concatenate([part[0] for part in parts], axis=1).astype(jnp.bfloat16)
        place = jnp.concatenate([part[1] for part in parts], axis=1).astype(jnp.bfloat16)
        for q in range(LAGS // ROWS):
            table_ref[o, q * ROWS:(q + 1) * ROWS, :] = jnp.where(place == jnp.bfloat16(q), stencil, jnp.bfloat16(0))

    def table_of(o):
        if o in stored:
            return table_ref[o]
        columns = []
        for a in range(across):
            stencil, place = entries(o, a)
            place = jnp.concatenate([place, place - 1.0], axis=0).astype(jnp.bfloat16)
            stencil = jnp.concatenate([stencil, stencil], axis=0).astype(jnp.bfloat16)
            columns.append(jnp.concatenate([
                jnp.where(place == jnp.bfloat16(2 * q), stencil, jnp.bfloat16(0)) for q in range(LAGS // BP)], axis=0))
        return jnp.concatenate(columns, axis=1)

    def widen_step(tile):
        columns = slice(tile * KT, (tile + 1) * KT)
        wide_ref[:, columns] = green_ref[:, columns].astype(jnp.float32)

    def spread_step(first, last, tile):
        pieces = []
        for o in range(first, last, 2):
            for h in range(KT // LANES):
                lanes = slice(tile * KT + h * LANES, tile * KT + (h + 1) * LANES)
                pair = jnp.concatenate([
                    jnp.broadcast_to(wide_ref[i:i + 1, lanes], (ROWS, LANES)) for i in (o, o + 1)], axis=0)
                pair = pair.astype(jnp.bfloat16) * diagonal
                pieces.append(jnp.concatenate([pair if i == h else empty for i in range(KT // LANES)], axis=1))
        product = jnp.dot(jnp.concatenate(pieces, axis=0), load_ref[tile * KT:(tile + 1) * KT, :],
                          preferred_element_type=jnp.float32)
        for o in range(first, last, 2):
            for i in range(2):
                start = (o - first) * BP + i * ROWS
                rows = jnp.concatenate([product[start + h * BP:start + h * BP + ROWS] for h in range(KT // LANES)], axis=0)
                block_ref[o + i, tile * BP:(tile + 1) * BP, :] = rows.astype(jnp.bfloat16)

    def lag_step(o):
        return jnp.dot(table_of(o), block_ref[o], preferred_element_type=jnp.float32)

    def shift(parts, amount):
        keep = lane >= amount
        rolled = [None if part is None else pltpu.roll(part, amount, 1) for part in parts]
        moved = [jnp.where(keep, rolled[0], 0.0)]
        for j in range(1, len(parts)):
            moved.append(jnp.where(keep, 0.0 if rolled[j] is None else rolled[j], rolled[j - 1]))
        return moved

    def add(left, right):
        return [l if r is None else l + r for l, r in zip(left, right)]

    def fold(left, right):
        totals = [[lagged[:ROWS, j * LANES:(j + 1) * LANES] for j in range(wide)] + [None] for lagged in (left, right)]
        for h in range(1, LAGS // ROWS):
            rows = slice(h * ROWS, (h + 1) * ROWS)
            keep = lane16 >= h * ROWS
            rolled = []
            for j in range(wide):
                lanes = slice(j * LANES, (j + 1) * LANES)
                both = jnp.concatenate([left[rows, lanes], right[rows, lanes]], axis=0).astype(jnp.bfloat16)
                rolled.append(pltpu.roll(both, h * ROWS, 1))
            none = jnp.zeros_like(rolled[0])
            moved = [jnp.where(keep, a, b) for a, b in zip(rolled + [none], [none] + rolled)]
            moved = [part.astype(jnp.float32) for part in moved]
            totals = [add([part[i * ROWS:(i + 1) * ROWS] for part in moved], totals[i]) for i in range(2)]
        return totals

    def merge(left, right, bit):
        clear = (row8 & bit) == 0
        stay, move = [], []
        for a, b in zip(left, right):
            stay.append(jnp.where(clear, a, pltpu.roll(b, bit, 0)))
            move.append(jnp.where(clear, pltpu.roll(a, ROWS - bit, 0), b))
        return add(shift(move, bit), stay)

    def gather(folded):
        bit = ROWS // 2
        while len(folded) > 1:
            half = len(folded) // 2
            folded = [merge(folded[i], folded[i + half], bit) for i in range(half)]
            bit //= 2
        return folded[0]

    spans = ((0, observers),)

    def main_copy(c, d):
        rows = slice(*spans[c])
        return pltpu.make_async_remote_copy(
            src_ref=main_out.at[rows],
            dst_ref=main_in.at[d - 1, rows],
            send_sem=main_send.at[c, d - 1], recv_sem=main_recv.at[c, d - 1],
            device_id={"panel": lax.rem(panel + d, panels)}, device_id_type=MESH)

    def tail_copy(c, d):
        rows = slice(*spans[c])
        return pltpu.make_async_remote_copy(
            src_ref=tail_out.at[rows],
            dst_ref=tail_in.at[d, rows],
            send_sem=tail_send.at[c, d], recv_sem=tail_recv.at[c, d],
            device_id={"panel": lax.rem(panel + d, panels), "slab": slab + 1}, device_id_type=MESH)

    def sum_rows(first):
        folded = []
        for o in range(first, first + ROWS, 2):
            folded += fold(lag_step(o), lag_step(o + 1))
        gathered = gather(folded)
        rows = slice(first, first + ROWS)
        for j in range(wide):
            lanes = slice(j * LANES, (j + 1) * LANES)
            part_ref[rows, lanes] = gathered[j]
            main_out[rows, lanes] = gathered[j].astype(jnp.bfloat16)
        tail_out[rows, :] = gathered[wide].astype(jnp.bfloat16)

    def send(c):
        for d in range(1, panels):
            main_copy(c, d).start()

        @pl.when(has_next)
        def _():
            for d in range(panels):
                tail_copy(c, d).start()

    waiting = list(stored)
    for c in range(len(SHARES)):
        for o in waiting[:len(stored) * TABLES[c] // sum(TABLES)]:
            table_step(o)
            waiting.remove(o)
        greens[c].wait()
        loads[c].wait()
        for tile in range(edges[c], edges[c + 1]):
            widen_step(tile)
            spread_step(0, observers, tile)
    for o in waiting:
        table_step(o)

    for c in range(len(spans)):
        for first in range(spans[c][0], spans[c][1], ROWS):
            sum_rows(first)
        if c == 0:
            pl.semaphore_wait(barrier, panels - 1 + panels * (has_next.astype(jnp.int32) + has_prev.astype(jnp.int32)))
        send(c)

    for c in range(len(spans)):
        rows = slice(*spans[c])
        total = part_ref[rows, :]
        for d in range(1, panels):
            main_copy(c, d).wait_recv()
            total = total + main_in[d - 1, rows, :].astype(jnp.float32)
        out_ref[rows, :] = total

        @pl.when(has_prev)
        def _():
            late = None
            for d in range(panels):
                tail_copy(c, d).wait_recv()
                term = tail_in[d, rows, :].astype(jnp.float32)
                late = term if late is None else late + term
            out_ref[rows, :LAGS] += late

    for c in range(len(spans)):
        for d in range(1, panels):
            main_copy(c, d).wait_send()

        @pl.when(has_next)
        def _():
            for d in range(panels):
                tail_copy(c, d).wait_send()


def shards(panels, slabs, loading, green, delays, offsets, live_groups):
    n_panels, samples = loading.shape
    observers = green.shape[0]
    blocks = delays.shape[1]
    peers = max(panels - 1, 1)
    anywhere = pl.BlockSpec(memory_space=pltpu.HBM)
    return pl.pallas_call(
        functools.partial(kernel, panels, slabs),
        out_shape=jax.ShapeDtypeStruct((observers, samples), jnp.float32),
        in_specs=[anywhere] * 5,
        out_specs=pl.BlockSpec(memory_space=pltpu.VMEM),
        scratch_shapes=[
            pltpu.SMEM((panels,), jnp.int32),
            pltpu.VMEM((n_panels, samples), jnp.bfloat16),
            pltpu.VMEM((observers, n_panels), jnp.bfloat16),
            pltpu.VMEM((observers, blocks), jnp.int32),
            pltpu.VMEM((observers, blocks), jnp.int32),
            pltpu.VMEM((observers, LAGS, blocks), jnp.bfloat16),
            pltpu.VMEM((observers, blocks, samples), jnp.bfloat16),
            pltpu.VMEM((observers, n_panels), jnp.float32),
            pltpu.VMEM((observers, samples), jnp.float32),
            pltpu.VMEM((observers, samples), jnp.bfloat16),
            pltpu.VMEM((observers, LAGS), jnp.bfloat16),
            pltpu.VMEM((peers, observers, samples), jnp.bfloat16),
            pltpu.VMEM((panels, observers, LAGS), jnp.bfloat16),
            pltpu.SemaphoreType.DMA((len(SHARES),)),
            pltpu.SemaphoreType.DMA((len(SHARES),)),
            pltpu.SemaphoreType.DMA((3,)),
            pltpu.SemaphoreType.DMA((2, peers)),
            pltpu.SemaphoreType.DMA((2, peers)),
            pltpu.SemaphoreType.DMA((2, panels)),
            pltpu.SemaphoreType.DMA((2, panels)),
        ],
        compiler_params=pltpu.CompilerParams(
            collective_id=0, has_side_effects=True, vmem_limit_bytes=40 * 2 ** 20),
        name="far_field",
    )(*(pltpu.with_memory_space_constraint(x, pltpu.HBM) for x in (live_groups, loading, green, delays, offsets)))


def solution(mesh):
    placed = (
        P(("case", "panel"), "slab"),
        P(("case", "obs"), "panel"),
        P(("case", "obs"), "panel"),
        P(("case", "obs"), "panel"),
        P("case"),
    )
    return jax.shard_map(
        functools.partial(shards, mesh.shape["panel"], mesh.shape["slab"]),
        mesh=mesh, in_specs=placed, out_specs=P(("case", "obs"), "slab"), check_vma=False,
    )
```

```python
import functools
import math

import jax
import jax.numpy as jnp
from jax import lax
from jax.experimental import pallas as pl
from jax.experimental.pallas import tpu as pltpu
from jax.sharding import PartitionSpec as P

BP = 16
GB = 128
LAGS = 128
TAPS = 8
STEPS = 8
KT = 256
LANES = 128
ROWS = 8
SHARES = (4, 12, 16)
TABLES = (1, 1, 1, 1)
LATE = 8
MESH = pl.DeviceIdType.MESH


def kernel(panels, slabs, live_hbm, load_hbm, green_hbm, delay_hbm, offset_hbm, out_ref,
           live_ref, load_ref, green_ref, delay_ref, offset_ref, table_ref, block_ref, wide_ref, part_ref,
           main_out, tail_out, main_in, tail_in, load_sem, green_sem, small_sem, main_send, main_recv, tail_send, tail_recv):
    panel = lax.axis_index("panel")
    slab = lax.axis_index("slab")
    n_panels, samples = load_hbm.shape
    observers = green_hbm.shape[0]
    blocks = delay_hbm.shape[1]
    tiles = n_panels // KT
    wide = samples // LANES
    across = blocks // LANES
    edges = [tiles * sum(SHARES[:c]) // sum(SHARES) for c in range(len(SHARES) + 1)]
    has_next = slab < slabs - 1
    has_prev = slab > 0

    smalls = [pltpu.make_async_copy(src, dst, small_sem.at[i]) for i, (src, dst) in enumerate(
        ((delay_hbm, delay_ref), (offset_hbm, offset_ref), (live_hbm, live_ref)))]
    for copy in smalls:
        copy.start()
    greens, loads = [], []
    for c in range(len(SHARES)):
        rows = pl.ds(edges[c] * KT, (edges[c + 1] - edges[c]) * KT)
        greens.append(pltpu.make_async_copy(green_hbm.at[:, rows], green_ref.at[:, rows], green_sem.at[c]))
        greens[-1].start()
        loads.append(pltpu.make_async_copy(load_hbm.at[rows, :], load_ref.at[rows, :], load_sem.at[c]))
        loads[-1].start()

    barrier = pltpu.get_barrier_semaphore()
    for d in range(1, panels):
        pl.semaphore_signal(barrier, inc=1, device_id={"panel": lax.rem(panel + d, panels)}, device_id_type=MESH)

    @pl.when(has_next)
    def _():
        for d in range(panels):
            pl.semaphore_signal(barrier, inc=1, device_id={
                "panel": lax.rem(panel + d, panels), "slab": slab + 1}, device_id_type=MESH)

    @pl.when(has_prev)
    def _():
        for d in range(panels):
            pl.semaphore_signal(barrier, inc=1, device_id={
                "panel": lax.rem(panel + d, panels), "slab": slab - 1}, device_id_type=MESH)

    lane = lax.broadcasted_iota(jnp.int32, (ROWS, LANES), 1)
    row8 = lax.broadcasted_iota(jnp.int32, (ROWS, LANES), 0)
    lane16 = lax.broadcasted_iota(jnp.int32, (BP, LANES), 1)
    row16 = lax.broadcasted_iota(jnp.int32, (BP, LANES), 0)
    diagonal = jnp.where(lane16 // BP == row16 % ROWS, 1.0, 0.0).astype(jnp.bfloat16)
    empty = jnp.zeros((BP, LANES), jnp.bfloat16)

    position = 3.0 + (lane // TAPS).astype(jnp.float32) * 0.125
    tap_of = lane % TAPS
    choice = jnp.ones((ROWS, LANES), jnp.float32)
    below = jnp.ones((ROWS, LANES), jnp.float32)
    for m in range(TAPS):
        here = tap_of == m
        choice = choice * jnp.where(here, 1.0, position - float(m))
        below = below * jnp.where(here, 1.0, (tap_of - m).astype(jnp.float32))
    choice = choice / below

    for copy in smalls:
        copy.wait()
    live = live_ref[panel]
    group_of = lax.broadcasted_iota(jnp.int32, (observers, blocks), 1) // GB
    delay_ref[...] = jnp.where(group_of < live, delay_ref[...], 4 * LAGS)
    offset_ref[...] = offset_ref[...] * TAPS

    stored = [o for o in range(observers) if o == 0 or o >= observers - LATE]

    def entries(o, a):
        lanes = slice(a * LANES, (a + 1) * LANES)
        delay = jnp.broadcast_to(delay_ref[o:o + 1, lanes], (ROWS, LANES))
        step = jnp.broadcast_to(offset_ref[o:o + 1, lanes], (ROWS, LANES))
        which = step + ((row8 - delay) & (ROWS - 1))
        stencil = jnp.take_along_axis(choice, which, axis=1, mode="promise_in_bounds")
        return stencil, ((delay + (ROWS - 1) - row8) >> 3).astype(jnp.float32)

    def table_step(o):
        parts = [entries(o, a) for a in range(across)]
        stencil = jnp.concatenate([part[0] for part in parts], axis=1).astype(jnp.bfloat16)
        place = jnp.concatenate([part[1] for part in parts], axis=1).astype(jnp.bfloat16)
        for q in range(LAGS // ROWS):
            table_ref[o, q * ROWS:(q + 1) * ROWS, :] = jnp.where(place == jnp.bfloat16(q), stencil, jnp.bfloat16(0))

    def table_of(o):
        if o in stored:
            return table_ref[o]
        columns = []
        for a in range(across):
            stencil, place = entries(o, a)
            place = jnp.concatenate([place, place - 1.0], axis=0).astype(jnp.bfloat16)
            stencil = jnp.concatenate([stencil, stencil], axis=0).astype(jnp.bfloat16)
            columns.append(jnp.concatenate([
                jnp.where(place == jnp.bfloat16(2 * q), stencil, jnp.bfloat16(0)) for q in range(LAGS // BP)], axis=0))
        return jnp.concatenate(columns, axis=1)

    def widen_step(tile):
        columns = slice(tile * KT, (tile + 1) * KT)
        wide_ref[:, columns] = green_ref[:, columns].astype(jnp.float32)

    def spread_step(first, last, tile):
        pieces = []
        for o in range(first, last, 2):
            for h in range(KT // LANES):
                lanes = slice(tile * KT + h * LANES, tile * KT + (h + 1) * LANES)
                pair = jnp.concatenate([
                    jnp.broadcast_to(wide_ref[i:i + 1, lanes], (ROWS, LANES)) for i in (o, o + 1)], axis=0)
                pair = pair.astype(jnp.bfloat16) * diagonal
                pieces.append(jnp.concatenate([pair if i == h else empty for i in range(KT // LANES)], axis=1))
        product = jnp.dot(jnp.concatenate(pieces, axis=0), load_ref[tile * KT:(tile + 1) * KT, :],
                          preferred_element_type=jnp.float32)
        for o in range(first, last, 2):
            for i in range(2):
                start = (o - first) * BP + i * ROWS
                rows = jnp.concatenate([product[start + h * BP:start + h * BP + ROWS] for h in range(KT // LANES)], axis=0)
                block_ref[o + i, tile * BP:(tile + 1) * BP, :] = rows.astype(jnp.bfloat16)

    def lag_step(o):
        return jnp.dot(table_of(o), block_ref[o], preferred_element_type=jnp.float32)

    def shift(parts, amount):
        keep = lane >= amount
        rolled = [None if part is None else pltpu.roll(part, amount, 1) for part in parts]
        moved = [jnp.where(keep, rolled[0], 0.0)]
        for j in range(1, len(parts)):
            moved.append(jnp.where(keep, 0.0 if rolled[j] is None else rolled[j], rolled[j - 1]))
        return moved

    def add(left, right):
        return [l if r is None else l + r for l, r in zip(left, right)]

    def fold(left, right):
        totals = [[lagged[:ROWS, j * LANES:(j + 1) * LANES] for j in range(wide)] + [None] for lagged in (left, right)]
        for h in range(1, LAGS // ROWS):
            rows = slice(h * ROWS, (h + 1) * ROWS)
            keep = lane16 >= h * ROWS
            rolled = []
            for j in range(wide):
                lanes = slice(j * LANES, (j + 1) * LANES)
                both = jnp.concatenate([left[rows, lanes], right[rows, lanes]], axis=0).astype(jnp.bfloat16)
                rolled.append(pltpu.roll(both, h * ROWS, 1))
            none = jnp.zeros_like(rolled[0])
            moved = [jnp.where(keep, a, b) for a, b in zip(rolled + [none], [none] + rolled)]
            moved = [part.astype(jnp.float32) for part in moved]
            totals = [add([part[i * ROWS:(i + 1) * ROWS] for part in moved], totals[i]) for i in range(2)]
        return totals

    def merge(left, right, bit):
        clear = (row8 & bit) == 0
        stay, move = [], []
        for a, b in zip(left, right):
            stay.append(jnp.where(clear, a, pltpu.roll(b, bit, 0)))
            move.append(jnp.where(clear, pltpu.roll(a, ROWS - bit, 0), b))
        return add(shift(move, bit), stay)

    def gather(first, bit):
        if bit == ROWS // 2:
            return merge(*fold(lag_step(first), lag_step(first + bit)), bit)
        return merge(gather(first, 2 * bit), gather(first + bit, 2 * bit), bit)

    spans = ((0, observers),)

    def main_copy(c, d):
        rows = slice(*spans[c])
        return pltpu.make_async_remote_copy(
            src_ref=main_out.at[rows],
            dst_ref=main_in.at[d - 1, rows],
            send_sem=main_send.at[c, d - 1], recv_sem=main_recv.at[c, d - 1],
            device_id={"panel": lax.rem(panel + d, panels)}, device_id_type=MESH)

    def tail_copy(c, d):
        rows = slice(*spans[c])
        return pltpu.make_async_remote_copy(
            src_ref=tail_out.at[rows],
            dst_ref=tail_in.at[d, rows],
            send_sem=tail_send.at[c, d], recv_sem=tail_recv.at[c, d],
            device_id={"panel": lax.rem(panel + d, panels), "slab": slab + 1}, device_id_type=MESH)

    def sum_rows(first):
        gathered = gather(first, 1)
        rows = slice(first, first + ROWS)
        for j in range(wide):
            lanes = slice(j * LANES, (j + 1) * LANES)
            part_ref[rows, lanes] = gathered[j]
            main_out[rows, lanes] = gathered[j].astype(jnp.bfloat16)
        tail_out[rows, :] = gathered[wide].astype(jnp.bfloat16)

    def send(c):
        for d in range(1, panels):
            main_copy(c, d).start()

        @pl.when(has_next)
        def _():
            for d in range(panels):
                tail_copy(c, d).start()

    waiting = list(stored)
    for c in range(len(SHARES)):
        for o in waiting[:len(stored) * TABLES[c] // sum(TABLES)]:
            table_step(o)
            waiting.remove(o)
        greens[c].wait()
        loads[c].wait()
        for tile in range(edges[c], edges[c + 1]):
            widen_step(tile)
            spread_step(0, observers, tile)
    for o in waiting:
        table_step(o)

    for c in range(len(spans)):
        for first in range(spans[c][0], spans[c][1], ROWS):
            sum_rows(first)
        if c == 0:
            pl.semaphore_wait(barrier, panels - 1 + panels * (has_next.astype(jnp.int32) + has_prev.astype(jnp.int32)))
        send(c)

    for c in range(len(spans)):
        rows = slice(*spans[c])
        total = part_ref[rows, :]
        for d in range(1, panels):
            main_copy(c, d).wait_recv()
            total = total + main_in[d - 1, rows, :].astype(jnp.float32)
        out_ref[rows, :] = total

        @pl.when(has_prev)
        def _():
            late = None
            for d in range(panels):
                tail_copy(c, d).wait_recv()
                term = tail_in[d, rows, :].astype(jnp.float32)
                late = term if late is None else late + term
            out_ref[rows, :LAGS] += late

    for c in range(len(spans)):
        for d in range(1, panels):
            main_copy(c, d).wait_send()

        @pl.when(has_next)
        def _():
            for d in range(panels):
                tail_copy(c, d).wait_send()


def shards(panels, slabs, loading, green, delays, offsets, live_groups):
    n_panels, samples = loading.shape
    observers = green.shape[0]
    blocks = delays.shape[1]
    peers = max(panels - 1, 1)
    anywhere = pl.BlockSpec(memory_space=pltpu.HBM)
    return pl.pallas_call(
        functools.partial(kernel, panels, slabs),
        out_shape=jax.ShapeDtypeStruct((observers, samples), jnp.float32),
        in_specs=[anywhere] * 5,
        out_specs=pl.BlockSpec(memory_space=pltpu.VMEM),
        scratch_shapes=[
            pltpu.SMEM((panels,), jnp.int32),
            pltpu.VMEM((n_panels, samples), jnp.bfloat16),
            pltpu.VMEM((observers, n_panels), jnp.bfloat16),
            pltpu.VMEM((observers, blocks), jnp.int32),
            pltpu.VMEM((observers, blocks), jnp.int32),
            pltpu.VMEM((observers, LAGS, blocks), jnp.bfloat16),
            pltpu.VMEM((observers, blocks, samples), jnp.bfloat16),
            pltpu.VMEM((observers, n_panels), jnp.float32),
            pltpu.VMEM((observers, samples), jnp.float32),
            pltpu.VMEM((observers, samples), jnp.bfloat16),
            pltpu.VMEM((observers, LAGS), jnp.bfloat16),
            pltpu.VMEM((peers, observers, samples), jnp.bfloat16),
            pltpu.VMEM((panels, observers, LAGS), jnp.bfloat16),
            pltpu.SemaphoreType.DMA((len(SHARES),)),
            pltpu.SemaphoreType.DMA((len(SHARES),)),
            pltpu.SemaphoreType.DMA((3,)),
            pltpu.SemaphoreType.DMA((2, peers)),
            pltpu.SemaphoreType.DMA((2, peers)),
            pltpu.SemaphoreType.DMA((2, panels)),
            pltpu.SemaphoreType.DMA((2, panels)),
        ],
        compiler_params=pltpu.CompilerParams(
            collective_id=0, has_side_effects=True, vmem_limit_bytes=40 * 2 ** 20),
        name="far_field",
    )(*(pltpu.with_memory_space_constraint(x, pltpu.HBM) for x in (live_groups, loading, green, delays, offsets)))


def solution(mesh):
    placed = (
        P(("case", "panel"), "slab"),
        P(("case", "obs"), "panel"),
        P(("case", "obs"), "panel"),
        P(("case", "obs"), "panel"),
        P("case"),
    )
    return jax.shard_map(
        functools.partial(shards, mesh.shape["panel"], mesh.shape["slab"]),
        mesh=mesh, in_specs=placed, out_specs=P(("case", "obs"), "slab"), check_vma=False,
    )
```
